32 devices in a mesh: cen: 8 (over y, x, core), grp: 4 (over z).
Axes of the slice: x: 2, y: 2, z: 4, core: 2. Of those that a mesh axis runs over, the one named last changes fastest.
Arguments:
- centers: bfloat16 [65536, 1024], P(('cen', 'grp')), may hold values from -2 to 2
- coefficients: float32 [65536, 256], P(('cen', 'grp')), may hold values from -0.09375 to 0.09375
- batch_index: int32 [256], P(('cen', 'grp')), may hold values from 0 to 65535, as said below
- batch_labels: float32 [256, 256], P(('cen', 'grp')), may hold values from -24 to 24
- nystrom_index: int32 [16384], P(('cen', 'grp')), may hold values from 0 to 65535, as said below
- eigenvectors: float32 [16384, 512], P(('cen', 'grp')), may hold values from -0.046875 to 0.046875
- eigen_weights: float32 [512], replicated, may hold values from 0.002 to 0.05
Outputs:
- residual: float32 [256, 256], P(('cen', 'grp'))
- correction: float32 [16384, 256], P(('cen', 'grp'))
The draws below stay inside these ranges and needn't reach their ends.
Inputs may be any that keep to these rules, and one draw needn't show every extreme that they name: `batch_index`: for each j, entries 8 * j to 8 * j + 7 are distinct rows among j * 2048 to j * 2048 + 2047. `nystrom_index`: for each j, entries 512 * j to 512 * j + 511 are distinct rows among j * 2048 to j * 2048 + 2047.
All inputs are finite; a program needn't handle non-finite values.
Results may differ from the reference program's by a relative error of at most 0.0003.
Values may be sent and summed in bfloat16 or wider, within the bound.
No kernel may reach another device: no remote copies, remote signals or barrier semaphores. Data moves between devices by JAX's collectives and lax.ppermute only.
A program may use at most 64 MiB of HBM per device.

```python
import math
import jax
import jax.numpy as jnp
from jax import lax

D = 1024
OUT = 256
EIG = 512
CEN_DEV = 2048
B_DEV = 8
NYS_DEV = 512
CENTERS = 65536
BATCH = 256
NYS = 16384


def pick_owned(key, per_shard):
    shards = CENTERS // CEN_DEV
    keys = jax.random.split(key, shards)
    picks = jax.vmap(lambda k: jax.random.permutation(k, CEN_DEV)[:per_shard])(keys)
    offsets = jnp.arange(shards, dtype=jnp.int32)[:, None] * CEN_DEV
    return (picks.astype(jnp.int32) + offsets).reshape(-1).astype(jnp.int32)


def draw_batch_index(key, part):
    return pick_owned(jax.random.fold_in(key, 11), B_DEV)


def draw_nystrom_index(key, part):
    return pick_owned(jax.random.fold_in(key, 23), NYS_DEV)


def draw_centers(key, part):
    base_key = jax.random.fold_in(key, 37)
    noise_key, direction_key, gain_key, cluster_key = jax.random.split(base_key, 4)
    clusters = 8
    noise = jax.random.normal(noise_key, (CENTERS, D), jnp.float32)
    row_gains = jax.random.uniform(gain_key, (CENTERS, 1), jnp.float32, -1.5, 1.5)
    directions = jax.random.normal(direction_key, (clusters, D), jnp.float32)
    cluster_id = jax.random.randint(cluster_key, (CENTERS,), 0, clusters)
    shared = jnp.take(directions, cluster_id, axis=0)
    factor = (128.0 / D) ** 0.5
    blended = factor * (0.70710678 * noise + 0.70710678 * row_gains * shared)
    return jnp.clip(blended, -2.0, 2.0).astype(jnp.bfloat16)


def levels(key, dims, pieces, least, high):
    gain = 1.0
    for position, shards_of in pieces:
        draws = jax.random.uniform(jax.random.fold_in(jax.random.fold_in(key, 6), position), (shards_of,), jnp.float32, least / len(pieces), high / len(pieces))
        gain = gain * jnp.repeat(jnp.exp(draws), dims[position] // shards_of).reshape((-1,) + (1,) * (len(dims) - 1 - position))
    return gain


def scatter_about(key, shape, deviation, reach, cuts=(), kind=jnp.bfloat16):
    entries = jax.random.normal(key, shape, jnp.float32) * deviation
    if len(cuts) > 0:
        entries = levels(key, shape, cuts, -0.22, 0.18) * entries
    return jnp.clip(entries, min=-reach, max=reach).astype(kind)


def setup_inputs(seed: int = 0) -> dict:
    streams_of = jax.random.split(jax.random.key(seed), 8)
    centers = draw_centers(jax.random.fold_in(streams_of[7], 71), 0)
    coefficients = scatter_about(streams_of[1], (CENTERS, OUT), (4 / CENTERS ** 0.5), 0.09375, ((0, 32),), jnp.float32)
    batch_index = draw_batch_index(jax.random.fold_in(streams_of[7], 71), 0)
    batch_labels = scatter_about(streams_of[3], (BATCH, OUT), 4.0, 24.0, ((0, 32),), jnp.float32)
    nystrom_index = draw_nystrom_index(jax.random.fold_in(streams_of[7], 71), 0)
    eigenvectors = scatter_about(streams_of[5], (NYS, EIG), NYS ** -0.5, 0.046875, ((0, 32),), jnp.float32)
    eigen_weights = jnp.clip(jnp.exp(jax.random.uniform(streams_of[6], (EIG,), jnp.float32, math.log(0.002), math.log(0.05))), 0.002, 0.05)
    return dict(centers=centers, coefficients=coefficients, batch_index=batch_index, batch_labels=batch_labels, nystrom_index=nystrom_index, eigenvectors=eigenvectors, eigen_weights=eigen_weights)


def reference(centers, coefficients, batch_index, batch_labels, nystrom_index, eigenvectors, eigen_weights):
    width = centers.shape[1]
    outputs = coefficients.shape[1]
    batch_x = jnp.take(centers, batch_index, axis=0)
    center_blocks = centers.reshape(-1, CEN_DEV, width)
    coef_blocks = coefficients.reshape(-1, CEN_DEV, outputs)

    def add_block(total, pair):
        block, coef = pair
        scores = lax.dot_general(batch_x, block, (((1,), (1,)), ((), ())), preferred_element_type=jnp.float32)
        kernel = jnp.exp(scores / 32.0)
        return total + jnp.dot(kernel, coef, precision=lax.Precision.HIGHEST, preferred_element_type=jnp.float32), None

    start_total = jnp.zeros((batch_x.shape[0], outputs), jnp.float32)
    predicted, unused = lax.scan(add_block, start_total, (center_blocks, coef_blocks))
    residual = predicted - batch_labels
    nystrom_x = jnp.take(centers, nystrom_index, axis=0).reshape(-1, NYS_DEV, width)

    def one_block(block):
        scores = lax.dot_general(block, batch_x, (((1,), (1,)), ((), ())), preferred_element_type=jnp.float32)
        nystrom_kernel = jnp.exp(scores / 32.0)
        return jnp.dot(nystrom_kernel, residual, precision=lax.Precision.HIGHEST, preferred_element_type=jnp.float32)

    local_products = lax.map(one_block, nystrom_x).reshape(-1, outputs)
    projected = jnp.dot(eigenvectors.T, local_products, precision=lax.Precision.HIGHEST, preferred_element_type=jnp.float32)
    correction = jnp.dot(eigenvectors, eigen_weights[:, None] * projected, precision=lax.Precision.HIGHEST, preferred_element_type=jnp.float32)
    return residual, correction
```

```python
import jax
import jax.numpy as jnp
from jax import lax
from jax.sharding import PartitionSpec as P

AXES = ("cen", "grp")


def exchange_stages(cen, grp):
    grp_bits = grp.bit_length() - 1
    bits = grp_bits + cen.bit_length() - 1
    stages = [(1 << b,) for b in range(grp_bits)]
    outer = list(range(grp_bits + 1, bits))
    for at in range(0, len(outer), 2):
        pair = [1 << b for b in outer[at : at + 2]]
        stages.append(tuple(pair) if len(pair) == 1 else (pair[0], pair[1], pair[0] | pair[1]))
    if bits > grp_bits:
        stages.append((1 << grp_bits,))
    return stages


def swap(x, offset, count):
    return lax.ppermute(x, AXES, [(i, i ^ offset) for i in range(count)])


def gather_rows(x, stages, count):
    for offsets in stages:
        x = jnp.concatenate([x] + [swap(x, k, count) for k in offsets], 0)
    return x


def reduce_rows(x, stages, count):
    for offsets in reversed(stages):
        rows = x.shape[0] // (len(offsets) + 1)
        own = x[:rows]
        for j, k in enumerate(offsets):
            own = own + swap(x[(j + 1) * rows : (j + 2) * rows], k, count)
        x = own
    return x


def dot3(left, right, dims):
    return lax.dot_general(
        left, right, (dims, ((), ())), precision=lax.Precision.HIGH, preferred_element_type=jnp.float32
    )


def inner_kernel(left, right):
    scores = lax.dot_general(left, right, (((1,), (1,)), ((), ())), preferred_element_type=jnp.float32)
    return jnp.exp(scores / 32.0)


def make_body(cen, grp):
    count = cen * grp
    stages = exchange_stages(cen, grp)

    def body(centers, coefficients, batch_index, batch_labels, nystrom_index, eigenvectors, eigen_weights):
        held = centers.shape[0]
        outs = coefficients.shape[1]
        owned = jnp.take(centers, batch_index % held, axis=0)
        nystrom_x = jnp.take(centers, nystrom_index % held, axis=0)
        batch_x = gather_rows(owned, stages, count)
        pred = dot3(inner_kernel(batch_x, centers), coefficients, ((1,), (0,)))
        cross = dot3(inner_kernel(batch_x, nystrom_x), eigenvectors, ((1,), (0,)))
        own = reduce_rows(jnp.concatenate([pred, cross], 1), stages, count)
        residual = own[:, :outs] - batch_labels
        both = gather_rows(jnp.concatenate([residual, own[:, outs:]], 1), stages, count)
        projected = dot3(both[:, outs:], both[:, :outs], ((0,), (0,)))
        correction = dot3(eigenvectors, eigen_weights[:, None] * projected, ((1,), (0,)))
        return residual, correction

    return body


def solution(mesh):
    rows = P(AXES, None)
    in_specs = (rows, rows, P(AXES), rows, P(AXES), rows, P())
    body = make_body(mesh.shape["cen"], mesh.shape["grp"])
    return jax.shard_map(body, mesh=mesh, in_specs=in_specs, out_specs=(rows, rows), check_vma=False)
```

```python
import jax
import jax.numpy as jnp
from jax import lax
from jax.experimental import pallas as pl
from jax.experimental.pallas import tpu as pltpu
from jax.sharding import PartitionSpec as P

AXES = ("cen", "grp")
VMEM = pl.BlockSpec(memory_space=pltpu.VMEM)
SMEM = pl.BlockSpec(memory_space=pltpu.SMEM)
HBM = pl.BlockSpec(memory_space=pltpu.HBM)
TILE = 8


def exchange_stages(cen, grp):
    grp_bits = grp.bit_length() - 1
    bits = grp_bits + cen.bit_length() - 1
    line = [1 << b for b in range(grp_bits)]
    upper = list(range(grp_bits + 1, bits))
    plane = []
    for at in range(0, len(upper), 2):
        pair = [1 << b for b in upper[at : at + 2]]
        plane.append(tuple(pair) if len(pair) == 1 else (pair[0], pair[1], pair[0] | pair[1]))
    if bits > grp_bits:
        plane.append((1 << grp_bits,))
    return line, plane


def swap(x, offset, count):
    return lax.ppermute(x, AXES, [(i, i ^ offset) for i in range(count)])


def gather_rows(x, stages, count):
    for offsets in stages:
        x = jnp.concatenate([x] + [swap(x, k, count) for k in offsets], 0)
    return x


def scatter_sum(x, stages, count):
    for offsets in reversed(stages):
        rows = x.shape[0] // (len(offsets) + 1)
        own = x[:rows]
        for j, k in enumerate(offsets):
            own = own + swap(x[(j + 1) * rows : (j + 2) * rows], k, count)
        x = own
    return x


def exchange_sum(x, line, count):
    slots = 1 << len(line)
    rows = x.shape[0] // slots
    for bit, k in enumerate(line):
        got = swap(x, k, count)
        got = jnp.concatenate([got[(s ^ (1 << bit)) * rows : ((s ^ (1 << bit)) + 1) * rows] for s in range(slots)], 0)
        x = x + got
    return x


def split(x):
    high = x.astype(jnp.bfloat16)
    return high, (x - high.astype(jnp.float32)).astype(jnp.bfloat16)


def product(left, right, contract):
    dims = (contract, ((), ()))
    dot = lambda a, b: lax.dot_general(a, b, dims, preferred_element_type=jnp.float32)
    return dot(left[0], right[0]) + (dot(left[0], right[1]) + dot(left[1], right[0]))


def own_rows_kernel(index, centers, out, blocks, sems):
    count = index.shape[0]
    held = centers.shape[0]
    copies = []
    for b in range(count):
        first = pl.multiple_of(lax.rem(index[b], held) // TILE * TILE, TILE)
        copy = pltpu.make_async_copy(centers.at[pl.ds(first, TILE)], blocks.at[b], sems.at[b])
        copy.start()
        copies.append(copy)
    row = lax.broadcasted_iota(jnp.int32, (TILE, centers.shape[1]), 0)
    picked = []
    for b in range(count):
        copies[b].wait()
        keep = row == lax.rem(index[b], TILE)
        picked.append(jnp.sum(jnp.where(keep, blocks[b].astype(jnp.float32), 0.0), 0, keepdims=True))
    out[...] = jnp.concatenate(picked, 0).astype(out.dtype)


def own_rows(index, centers):
    count, width = index.shape[0], centers.shape[1]
    return pl.pallas_call(
        own_rows_kernel,
        out_shape=jax.ShapeDtypeStruct((count, width), centers.dtype),
        in_specs=[SMEM, HBM],
        out_specs=VMEM,
        scratch_shapes=[pltpu.VMEM((count, TILE, width), centers.dtype), pltpu.SemaphoreType.DMA((count,))],
        compiler_params=pltpu.CompilerParams(vmem_limit_bytes=1 << 20),
        name="own_rows",
    )(index, pltpu.with_memory_space_constraint(centers, pltpu.HBM))


def scores_exp(batch, rows):
    scores = lax.dot_general(batch, rows, (((1,), (1,)), ((), ())), preferred_element_type=jnp.float32)
    return jnp.exp(scores / 32.0)


def partial_kernel(batch, centers, stored, index, eigenvectors, labels, out, high, low, coefficients, sem):
    fetch = pltpu.make_async_copy(stored, coefficients, sem)
    fetch.start()
    held, outs = coefficients.shape
    own, points = labels.shape[0], eigenvectors.shape[0]
    block, step = high.shape[0], min(512, held)
    local = lax.rem(index[...], held)
    for first in range(0, batch.shape[0], block):
        rows = slice(first, first + block)
        total = jnp.zeros((block, outs), jnp.float32)
        for at in range(0, held, step):
            high[:, at : at + step], low[:, at : at + step] = split(scores_exp(batch[rows], centers[at : at + step]))
        if first == 0:
            fetch.wait()
        for at in range(0, held, step):
            part = high[:, at : at + step], low[:, at : at + step]
            total = total + product(part, split(coefficients[at : at + step]), ((1,), (0,)))
        picked = [jnp.zeros((block, points), jnp.float32)] * 2
        for at in range(0, held, step):
            row = lax.broadcasted_iota(jnp.int32, (step, points), 0) + at
            mark = jnp.where(row == local, 1.0, 0.0).astype(jnp.bfloat16)
            picked = [
                p + jnp.dot(k[:, at : at + step], mark, preferred_element_type=jnp.float32)
                for p, k in zip(picked, (high, low))
            ]
        picked = [p.astype(jnp.bfloat16) for p in picked]
        out[rows, outs:] = product(picked, split(eigenvectors[...]), ((1,), (0,)))
        out[rows, :outs] = total
        if first == 0:
            out[:own, :outs] = total[:own] - labels[...]


def partial_sums(batch, centers, coefficients, index, eigenvectors, labels):
    width = coefficients.shape[1] + eigenvectors.shape[1]
    block = min(256, batch.shape[0])
    parts = pltpu.VMEM((block, centers.shape[0]), jnp.bfloat16)
    return pl.pallas_call(
        partial_kernel,
        out_shape=jax.ShapeDtypeStruct((batch.shape[0], width), jnp.float32),
        in_specs=[VMEM, VMEM, HBM, VMEM, VMEM, VMEM],
        out_specs=VMEM,
        scratch_shapes=[parts, parts, pltpu.VMEM(coefficients.shape, jnp.float32), pltpu.SemaphoreType.DMA],
        compiler_params=pltpu.CompilerParams(vmem_limit_bytes=24 << 20),
        name="partial_sums",
    )(batch, centers, pltpu.with_memory_space_constraint(coefficients, pltpu.HBM), index, eigenvectors, labels)


def correction_kernel(both, eigenvectors, weights, residual, correction):
    outs = correction.shape[1]
    residual[...] = both[: residual.shape[0], :outs]
    projected = product(split(both[:, outs:] * weights[...]), split(both[:, :outs]), ((0,), (0,)))
    correction[...] = product(split(eigenvectors[...]), split(projected), ((1,), (0,)))


def corrections(both, eigenvectors, weights, own, outs):
    return pl.pallas_call(
        correction_kernel,
        out_shape=(
            jax.ShapeDtypeStruct((own, outs), jnp.float32),
            jax.ShapeDtypeStruct((eigenvectors.shape[0], outs), jnp.float32),
        ),
        in_specs=[VMEM] * 3,
        out_specs=(VMEM, VMEM),
        compiler_params=pltpu.CompilerParams(vmem_limit_bytes=8 << 20),
        name="corrections",
    )(both, eigenvectors, weights)


def make_body(cen, grp):
    count = cen * grp
    line, plane = exchange_stages(cen, grp)

    def body(centers, coefficients, batch_index, batch_labels, nystrom_index, eigenvectors, eigen_weights):
        owned = own_rows(batch_index, centers)
        batch_x = gather_rows(owned, [(k,) for k in line] + plane, count)
        partial = partial_sums(batch_x, centers, coefficients, nystrom_index[None, :], eigenvectors, batch_labels)
        summed = exchange_sum(scatter_sum(partial, plane, count), line, count)
        both = gather_rows(summed, plane, count)
        own, outs = batch_labels.shape
        return corrections(both, eigenvectors, eigen_weights[None, :], own, outs)

    return body


def solution(mesh):
    rows = P(AXES, None)
    in_specs = (rows, rows, P(AXES), rows, P(AXES), rows, P())
    body = make_body(mesh.shape["cen"], mesh.shape["grp"])
    return jax.shard_map(body, mesh=mesh, in_specs=in_specs, out_specs=(rows, rows), check_vma=False)
```

```python
import jax
import jax.numpy as jnp
from jax import lax
from jax.experimental import pallas as pl
from jax.experimental.pallas import tpu as pltpu
from jax.sharding import PartitionSpec as P

AXES = ("cen", "grp")
VMEM = pl.BlockSpec(memory_space=pltpu.VMEM)
SMEM = pl.BlockSpec(memory_space=pltpu.SMEM)
HBM = pl.BlockSpec(memory_space=pltpu.HBM)
TILE = 8
LANES = 128
MIB = 1 << 20


def exchange_stages(cen, grp):
    grp_bits = grp.bit_length() - 1
    bits = grp_bits + cen.bit_length() - 1
    line = [1 << b for b in range(grp_bits)]
    upper = list(range(grp_bits + 1, bits))
    plane = []
    for at in range(0, len(upper), 2):
        pair = [1 << b for b in upper[at : at + 2]]
        plane.append(tuple(pair) if len(pair) == 1 else (pair[0], pair[1], pair[0] | pair[1]))
    if bits > grp_bits:
        plane.append((1 << grp_bits,))
    return line, plane


def swap(x, offset, count):
    return lax.ppermute(x, AXES, [(i, i ^ offset) for i in range(count)])


def gather_rows(x, stages, count):
    for offsets in stages:
        x = jnp.concatenate([x] + [swap(x, k, count) for k in offsets], 0)
    return x


def scatter_sum(x, stages, count):
    for offsets in reversed(stages):
        rows = x.shape[0] // (len(offsets) + 1)
        own = x[:rows]
        for j, k in enumerate(offsets):
            own = own + swap(x[(j + 1) * rows : (j + 2) * rows], k, count)
        x = own
    return x


def exchange_sum(x, line, count):
    slots = 1 << len(line)
    rows = x.shape[0] // slots
    for bit, k in enumerate(line):
        got = swap(x, k, count)
        got = jnp.concatenate([got[(s ^ (1 << bit)) * rows : ((s ^ (1 << bit)) + 1) * rows] for s in range(slots)], 0)
        x = x + got
    return x


def split(x):
    high = x.astype(jnp.bfloat16)
    return high, (x - high.astype(jnp.float32)).astype(jnp.bfloat16)


def dot(left, right, contract=((1,), (0,))):
    return lax.dot_general(left, right, (contract, ((), ())), preferred_element_type=jnp.float32)


def call(kernel, out_shape, in_specs, operands, scratch=(), limit=16 * MIB):
    return pl.pallas_call(
        kernel,
        out_shape=out_shape,
        in_specs=in_specs,
        out_specs=jax.tree.map(lambda _: VMEM, out_shape),
        scratch_shapes=scratch,
        compiler_params=pltpu.CompilerParams(vmem_limit_bytes=limit),
    )(*operands)


def own_rows_kernel(index, centers, out, blocks, sems):
    count = index.shape[0]
    held = centers.shape[0]
    copies = []
    for b in range(count):
        first = pl.multiple_of(lax.rem(index[b], held) // TILE * TILE, TILE)
        copy = pltpu.make_async_copy(centers.at[pl.ds(first, TILE)], blocks.at[b], sems.at[b])
        copy.start()
        copies.append(copy)
    row = lax.broadcasted_iota(jnp.int32, (TILE, centers.shape[1]), 0)
    picked = []
    for b in range(count):
        copies[b].wait()
        keep = row == lax.rem(index[b], TILE)
        picked.append(jnp.sum(jnp.where(keep, blocks[b].astype(jnp.float32), 0.0), 0, keepdims=True))
    out[...] = jnp.concatenate(picked, 0).astype(out.dtype)


def own_rows(index, centers):
    count, width = index.shape[0], centers.shape[1]
    return call(
        own_rows_kernel,
        jax.ShapeDtypeStruct((count, width), centers.dtype),
        [SMEM, HBM],
        (index, pltpu.with_memory_space_constraint(centers, pltpu.HBM)),
        [pltpu.VMEM((count, TILE, width), centers.dtype), pltpu.SemaphoreType.DMA((count,))],
        MIB,
    )


def prep_pieces_kernel(coefficients, eigenvectors, coef_t, eigen_t, eigen):
    for source, target in ((coefficients, coef_t), (eigenvectors, eigen_t)):
        width = source.shape[1]
        high, low = split(source[...].T)
        target[:width] = high
        target[width:] = low
    rows = eigenvectors.shape[0]
    eigen[:rows], eigen[rows:] = split(eigenvectors[...])


def prep_pieces(coefficients, eigenvectors):
    held, outs = coefficients.shape
    points, eig = eigenvectors.shape
    shapes = ((2 * outs, held), (2 * eig, points), (2 * points, eig))
    return call(
        prep_pieces_kernel,
        tuple(jax.ShapeDtypeStruct(s, jnp.bfloat16) for s in shapes),
        [VMEM] * 2,
        (coefficients, eigenvectors),
    )


def prep_rows_kernel(index, centers, out, mark):
    held, points = centers.shape[0], index.shape[1]
    local = lax.rem(index[...], held).astype(jnp.float32)
    column = jnp.broadcast_to(local, (LANES, points)).T.astype(jnp.int32)
    lane = lax.broadcasted_iota(jnp.int32, (points, LANES), 1)
    for at in range(0, held, LANES):
        mark[:, at : at + LANES] = jnp.where(lane + at == column, 1.0, 0.0).astype(jnp.bfloat16)
    out[...] = dot(mark[...], centers[...]).astype(out.dtype)


def prep_rows(index, centers):
    points = index.shape[1]
    return call(
        prep_rows_kernel,
        jax.ShapeDtypeStruct((points, centers.shape[1]), centers.dtype),
        [VMEM] * 2,
        (index, centers),
        [pltpu.VMEM((points, centers.shape[0]), jnp.bfloat16)],
    )


def partial_kernel(batch, centers, nystrom, coef_t, eigen_t, labels, out, high, low):
    outs, own = labels.shape[1], labels.shape[0]
    block, step = high.shape[1], 256
    for first in range(0, batch.shape[0], block):
        rows = slice(first, first + block)
        columns = batch[rows]

        def weighted(points, pieces):
            count, width = points.shape[0], pieces.shape[0] // 2
            for at in range(0, count, step):
                scores = dot(points[at : at + step], columns, ((1,), (1,)))
                high[at : at + step], low[at : at + step] = split(jnp.exp(scores / 32.0))
            both = dot(pieces[...], high[:count])
            return (both[:width] + (both[width:] + dot(pieces[:width], low[:count]))).T

        predicted = weighted(centers, coef_t)
        out[rows, :outs] = predicted
        if first == 0:
            out[:own, :outs] = predicted[:own] - labels[...]
        out[rows, outs:] = weighted(nystrom, eigen_t)


def partial_sums(batch, centers, nystrom, coef_t, eigen_t, labels):
    width = coef_t.shape[0] // 2 + eigen_t.shape[0] // 2
    block = min(256, batch.shape[0])
    parts = pltpu.VMEM((max(centers.shape[0], nystrom.shape[0]), block), jnp.bfloat16)
    return call(
        partial_kernel,
        jax.ShapeDtypeStruct((batch.shape[0], width), jnp.float32),
        [VMEM] * 6,
        (batch, centers, nystrom, coef_t, eigen_t, labels),
        [parts, parts],
        24 * MIB,
    )


def correction_kernel(both, eigen, weights, residual, correction):
    outs = correction.shape[1]
    residual[...] = both[: residual.shape[0], :outs]
    high, low = split(both[:, :outs])
    cross = split(both[:, outs:] * weights[...])
    first = ((0,), (0,))
    projected = split(dot(cross[0], high, first) + (dot(cross[0], low, first) + dot(cross[1], high, first)))
    points = eigen.shape[0] // 2
    wide = dot(eigen[...], projected[0])
    correction[...] = wide[:points] + (wide[points:] + dot(eigen[:points], projected[1]))


def corrections(both, eigen, weights, own, outs):
    shapes = ((own, outs), (eigen.shape[0] // 2, outs))
    return call(
        correction_kernel,
        tuple(jax.ShapeDtypeStruct(s, jnp.float32) for s in shapes),
        [VMEM] * 3,
        (both, eigen, weights),
        limit=8 * MIB,
    )


def make_body(line, plane, count):
    def body(centers, coefficients, batch_index, batch_labels, nystrom_index, eigenvectors, eigen_weights):
        owned = own_rows(batch_index, centers)
        coef_t, eigen_t, eigen = prep_pieces(coefficients, eigenvectors)
        nystrom_x = prep_rows(nystrom_index[None, :], centers)
        batch_x = gather_rows(owned, [(k,) for k in line] + plane, count)
        partial = partial_sums(batch_x, centers, nystrom_x, coef_t, eigen_t, batch_labels)
        summed = exchange_sum(scatter_sum(partial, plane, count), line, count)
        both = gather_rows(summed, plane, count)
        own, outs = batch_labels.shape
        return corrections(both, eigen, eigen_weights[None, :], own, outs)

    return body


def solution(mesh):
    rows = P(AXES, None)
    in_specs = (rows, rows, P(AXES), rows, P(AXES), rows, P())
    line, plane = exchange_stages(mesh.shape["cen"], mesh.shape["grp"])
    body = make_body(line, plane, mesh.shape["cen"] * mesh.shape["grp"])
    return jax.shard_map(body, mesh=mesh, in_specs=in_specs, out_specs=(rows, rows), check_vma=False)
```
